128 devices in a mesh: dp: 2 (over core), expert: 64 (over x, y, z).
Axes of the slice: x: 4, y: 4, z: 4, core: 2. Of those that a mesh axis runs over, the one named last changes fastest.
Arguments:
- tokens: bfloat16 [8192, 4096], P(('dp', 'expert')), may hold values from -6 to 6
- expert_ids: int32 [8192, 8], P(('dp', 'expert')), may hold values from 0 to 63, all different within a row; in each aligned block of 64 rows (0 to 63, 64 to 127, ...) at most 12 rows name the same one
- gate_num: int32 [8192, 8], P(('dp', 'expert')), may hold values from 1 to 1024
- w_gate: bfloat16 [64, 4096, 1536], P('expert', None, 'dp'), may hold values from -0.09375 to 0.09375
- w_up: bfloat16 [64, 4096, 1536], P('expert', None, 'dp'), may hold values from -0.09375 to 0.09375
- w_down: bfloat16 [64, 1536, 4096], P('expert', 'dp'), may hold values from -0.15625 to 0.15625
Outputs:
- mixed: bfloat16 [8192, 4096], P(('dp', 'expert'))
The draws below stay inside these ranges and needn't reach their ends.
Inputs may be any that keep to these rules, and one draw needn't show every extreme that they name: `expert_ids`: each row names 8 different experts; among the 64 rows of one device no expert is named more than 12 times, a bound that some block reaches.
All inputs are finite; a program needn't handle non-finite values.
Results may differ from the reference program's by a relative error of at most 0.0057.
Values may be sent and summed in bfloat16 or wider, within the bound.
No kernel may reach another device: no remote copies, remote signals or barrier semaphores. Data moves between devices by JAX's collectives and lax.ppermute only.
A program may use at most 192 MiB of HBM per device.

```python
import math
import jax
import jax.numpy as jnp
import numpy as np
from jax import lax

D = 4096
FF = 1536
TOP = 8
GATE_DEN = 1024
TOK_DEV = 64
EXPERTS = 64
CAP = 12
TOKENS = 8192


def with_ends(drawn, key, smallest, top_value):
    longest = drawn.shape.index(max(drawn.shape))
    spots = []
    for shift in (0, 1):
        where = [jax.random.randint(jax.random.fold_in(key, axis), (), 0, length) for axis, length in enumerate(drawn.shape)]
        where[longest] = (where[longest] + shift) % drawn.shape[longest]
        spots.append(tuple(where))
    return drawn.at[spots[0]].set(smallest).at[spots[1]].set(top_value)


def block_levels(stream_key, extent, cuts, least, largest):
    loudness, own = 1.0, jax.random.fold_in(stream_key, 6)
    for dim, blocks in cuts:
        heights = jnp.exp(jax.random.uniform(jax.random.fold_in(own, dim), (blocks,), jnp.float32, least / len(cuts), largest / len(cuts)))
        loudness = loudness * jnp.repeat(heights, extent[dim] // blocks).reshape([-1 if axis == dim else 1 for axis in range(len(extent))])
    return loudness


def assign_block(own_key, own, number, rows, count, top, reach, slope):
    sequence = jax.random.permutation(own_key, count)
    heavy_load, ordinary = load_shares(count, rows * top, reach, slope, True), load_shares(count, rows * top, reach, slope, False)
    places = jnp.arange(count)

    def named(tallies, rotation):
        used = int((tallies > 0).sum())
        fixed = max(1, used // 4)
        moved = fixed + (places - fixed + rotation * (used - fixed)) % max(1, count - fixed)
        return jnp.zeros((count,), jnp.int32).at[sequence[jnp.where(places < fixed, places, moved)]].set(jnp.asarray(tallies, jnp.int32))

    tallies = jnp.where(number % 4 == 0, named(heavy_load, number // 4), named(ordinary, number - number // 4 - 1))
    mixed = jax.random.permutation(jax.random.fold_in(own, 3), count)
    source_of, receiver = mixed[0:count // 2 * 2:2], mixed[1:count // 2 * 2:2]
    margin = jnp.minimum(tallies[source_of] - 1, reach - tallies[receiver]) // 2
    margin = jnp.where((source_of == sequence[0]) | (receiver == sequence[0]) | (tallies[receiver] == 0), 0, jnp.maximum(margin, 0))
    moved = jax.random.randint(jax.random.fold_in(own, 4), (count // 2,), 0, 1 << 20) % (margin + 1)
    tallies = tallies.at[source_of].add(-moved).at[receiver].add(moved)
    items = jnp.searchsorted(jnp.cumsum(tallies), jnp.arange(rows * top), side="right").astype(jnp.int32)
    listing = items.reshape(top, rows).T
    listing = listing[jax.random.permutation(jax.random.fold_in(own, 1), rows)]
    rotation = jax.random.randint(jax.random.fold_in(own, 2), (rows, 1), 0, top)
    return jnp.take_along_axis(listing, (jnp.arange(top)[None, :] + rotation) % top, axis=1)


def load_shares(amount, total, limit, slope, full):
    loads = [(1 << 20) // math.isqrt(grade ** slope) + 1 for grade in range(1, amount + 1)]
    largest = limit if full else min(limit, max(-(-total // amount), total * loads[0] // sum(loads)))
    least = 1 if total - largest >= amount - 1 else 0
    holding, rest = [largest] + [least] * (amount - 1), total - largest - least * (amount - 1)
    while rest > 0:
        movable = [i for i in range(1, amount) if holding[i] < largest] or [i for i in range(1, amount) if holding[i] < limit]
        pool, remaining = sum([loads[i] for i in movable]), rest
        for i in movable:
            more = min(limit - holding[i], max(1, remaining * loads[i] // pool), rest)
            holding[i] = holding[i] + more
            rest = rest - more
    return np.array(holding)


def gaussian(key, dims, deviation, most, shards=(), kind=jnp.bfloat16):
    factor_of = block_levels(key, dims, shards, -0.22, 0.18) if shards else 1.0
    entries = jax.random.normal(key, dims, jnp.float32) * deviation * factor_of
    return jnp.minimum(jnp.maximum(entries, -most), most).astype(kind)


def setup_inputs(seed: int = 0) -> dict:
    seeds = jax.random.split(jax.random.key(seed), 7)
    tokens = gaussian(seeds[0], (TOKENS, D), 1.0, 6.0, ((0, 128),))
    expert_ids_keys = jax.random.split(jax.random.fold_in(seeds[1], 1), TOKENS // TOK_DEV)
    expert_ids_turns = jax.random.permutation(jax.random.fold_in(seeds[1], 3), TOKENS // TOK_DEV)
    expert_ids = jax.vmap(lambda own, number: assign_block(jax.random.fold_in(seeds[1], 2), own, number, TOK_DEV, EXPERTS, TOP, CAP, 2))(expert_ids_keys, expert_ids_turns).reshape((TOKENS, TOP))
    gate_num = with_ends(jax.random.randint(seeds[2], (TOKENS, TOP), 1, GATE_DEN + 1), jax.random.fold_in(seeds[2], 1), 1, GATE_DEN).astype(jnp.int32)
    w_gate = gaussian(seeds[3], (EXPERTS, D, FF), D ** -0.5, 0.09375, ((0, 64), (2, 2)))
    w_up = gaussian(seeds[4], (EXPERTS, D, FF), D ** -0.5, 0.09375, ((0, 64), (2, 2)))
    w_down = gaussian(seeds[5], (EXPERTS, FF, D), FF ** -0.5, 0.15625, ((0, 64), (1, 2)))
    return dict(tokens=tokens, expert_ids=expert_ids, gate_num=gate_num, w_gate=w_gate, w_up=w_up, w_down=w_down)


def expert_block(block_rows, gate_mat, up_mat, down_mat):
    gate_part = jnp.dot(block_rows, gate_mat, preferred_element_type=jnp.float32)
    up_part = jnp.dot(block_rows, up_mat, preferred_element_type=jnp.float32)
    hidden = (jax.nn.silu(gate_part) * up_part).astype(jnp.bfloat16)
    return jnp.dot(hidden, down_mat, preferred_element_type=jnp.float32).astype(jnp.bfloat16)


def reference(tokens, expert_ids, gate_num, w_gate, w_up, w_down):
    assigned = TOKENS * TOP
    flat_expert = expert_ids.reshape(-1).astype(jnp.int32)
    flat_token = (jnp.arange(assigned, dtype=jnp.int32) // TOP).astype(jnp.int32)
    flat_gate = gate_num.reshape(-1).astype(jnp.float32) / GATE_DEN
    per_expert = jnp.sum((flat_expert[:, None] == jnp.arange(EXPERTS, dtype=jnp.int32)[None, :]).astype(jnp.int32), axis=0)
    padded = ((per_expert + 127) // 128) * 128
    starts = (jnp.cumsum(padded) - padded).astype(jnp.int32)
    firsts = (jnp.cumsum(per_expert) - per_expert).astype(jnp.int32)
    order = jnp.argsort(flat_expert, stable=True).astype(jnp.int32)
    sorted_expert = flat_expert[order]
    within = jnp.arange(assigned, dtype=jnp.int32) - firsts[sorted_expert]
    target = (starts[sorted_expert] + within).astype(jnp.int32)
    blocks = (assigned + 127) // 128 + EXPERTS
    row_token = jnp.zeros((blocks * 128,), jnp.int32).at[target].set(flat_token[order])
    row_gate = jnp.zeros((blocks * 128,), jnp.float32).at[target].set(flat_gate[order])
    block_start = jnp.arange(blocks, dtype=jnp.int32) * 128
    block_expert = (jnp.sum((starts[None, :] <= block_start[:, None]).astype(jnp.int32), axis=1) - 1).astype(jnp.int32)

    def add_block(total_out, index):
        start = (index * 128).astype(jnp.int32)
        rows_token = lax.dynamic_slice_in_dim(row_token, start, 128)
        gates = lax.dynamic_slice_in_dim(row_gate, start, 128)
        owner = block_expert[index]
        result = expert_block(tokens[rows_token], w_gate[owner], w_up[owner], w_down[owner])
        return total_out.at[rows_token].add(gates[:, None] * result.astype(jnp.float32)), None

    total_out, _ = lax.scan(add_block, jnp.zeros((TOKENS, D), jnp.float32), jnp.arange(blocks, dtype=jnp.int32))
    return total_out.astype(jnp.bfloat16)
```

```python
import jax
import jax.numpy as jnp
from jax import lax
from jax.sharding import PartitionSpec as P

MAIN = 8
EXTRA = 4


def mm(a, b):
    return jnp.dot(a, b, preferred_element_type=jnp.float32)


def tmm(a, b):
    return lax.dot_general(a, b, (((0,), (0,)), ((), ())), preferred_element_type=jnp.float32)


def exchange(rows):
    return lax.all_to_all(rows, "expert", split_axis=0, concat_axis=0, tiled=True)


def expert_rows(rows, own, other):
    total = None
    for gate_mat, up_mat, down_mat in (own, other):
        hidden = (jax.nn.silu(mm(rows, gate_mat)) * mm(rows, up_mat)).astype(jnp.bfloat16)
        part = mm(hidden, down_mat)
        total = part if total is None else total + part
    return total.astype(jnp.bfloat16)


def body(tokens, expert_ids, gate_num, w_gate, w_up, w_down):
    tok, width = tokens.shape
    half = width // 2
    experts = lax.axis_size("expert")
    bf16 = jnp.bfloat16
    own = (w_gate[0], w_up[0], w_down[0])
    other = tuple(lax.ppermute(w, "dp", [(0, 1), (1, 0)]) for w in own)

    ids = expert_ids.T[None]
    hits = ids == jnp.arange(experts, dtype=jnp.int32)[:, None, None]
    member = jnp.any(hits, axis=1)
    numer = jnp.sum(jnp.where(hits, gate_num.T[None], 0), axis=1)
    before = jnp.arange(tok)[:, None] < jnp.arange(tok)[None, :]
    rank_of = mm(member.astype(bf16), before.astype(bf16)).astype(jnp.int32)
    rank_of = jnp.where(member, rank_of, -1)

    main_slot = jnp.arange(MAIN, dtype=jnp.int32)[None, :, None]
    main_place = rank_of[:, None, :] == main_slot
    outgoing = mm(main_place.reshape(experts * MAIN, tok).astype(bf16), tokens).astype(bf16)
    main_in = exchange(outgoing.reshape(experts, MAIN, width))

    line = jnp.arange(2 * EXTRA, dtype=jnp.int32)[None, :, None]
    column_half = jnp.arange(2 * tok, dtype=jnp.int32)[None, None, :] // tok
    rank_twice = jnp.concatenate([rank_of, rank_of], axis=1)[:, None, :]
    extra_place = (rank_twice == MAIN + line % EXTRA) & (line // EXTRA == column_half)
    halves = jnp.concatenate([tokens[:, :half], tokens[:, half:]], axis=0)
    extra_out = mm(extra_place.reshape(experts * 2 * EXTRA, 2 * tok).astype(bf16), halves).astype(bf16)
    extra_in = exchange(extra_out.reshape(experts, 2 * EXTRA, half))

    main_res = expert_rows(main_in.reshape(experts * MAIN, width), own, other)
    main_back = exchange(main_res.reshape(experts, MAIN, width))

    extra_rows = extra_in.reshape(experts, 2, EXTRA, half).transpose(0, 2, 1, 3).reshape(experts * EXTRA, width)
    extra_res = expert_rows(extra_rows, own, other)
    extra_res = extra_res.reshape(experts, EXTRA, 2, half).transpose(0, 2, 1, 3)
    extra_back = exchange(extra_res.reshape(experts, 2 * EXTRA, half))

    high, low = numer // 8, numer % 8
    main_gate = jnp.concatenate(
        [jnp.where(main_place, part[:, None, :], 0) for part in (high, low)], axis=2
    ).reshape(experts * MAIN, 2 * tok)
    main_sum = tmm(main_gate.astype(bf16), main_back.reshape(experts * MAIN, width))
    extra_gate = jnp.concatenate(
        [jnp.where(extra_place, jnp.concatenate([part, part], axis=1)[:, None, :], 0) for part in (high, low)], axis=2
    ).reshape(experts * 2 * EXTRA, 4 * tok)
    extra_sum = tmm(extra_gate.astype(bf16), extra_back.reshape(experts * 2 * EXTRA, half))
    main_sum = 8.0 * main_sum[:tok] + main_sum[tok:]
    extra_sum = 8.0 * extra_sum[: 2 * tok] + extra_sum[2 * tok :]
    extra_sum = jnp.concatenate([extra_sum[:tok], extra_sum[tok:]], axis=1)
    return ((main_sum + extra_sum) * (1.0 / 1024)).astype(bf16)


def solution(mesh):
    in_specs = (
        P(("dp", "expert"), None),
        P(("dp", "expert"), None),
        P(("dp", "expert"), None),
        P("expert", None, "dp"),
        P("expert", None, "dp"),
        P("expert", "dp", None),
    )
    out_specs = P(("dp", "expert"), None)
    return jax.shard_map(body, mesh=mesh, in_specs=in_specs, out_specs=out_specs, check_vma=False)
```

```python
import jax
import jax.numpy as jnp
from jax import lax
from jax.experimental import pallas as pl
from jax.experimental.pallas import tpu as pltpu
from jax.sharding import PartitionSpec as P

MAIN = 8
EXTRA = 4


def mm(a, b):
    return jnp.dot(a, b, preferred_element_type=jnp.float32)


def tmm(a, b):
    return lax.dot_general(a, b, (((0,), (0,)), ((), ())), preferred_element_type=jnp.float32)


def exchange(rows):
    return lax.all_to_all(rows, "expert", split_axis=0, concat_axis=0, tiled=True)


FBLK = 256
DBLK = 512


def expert_kernel(x_ref, g0_ref, g1_ref, u0_ref, u1_ref, d0_ref, d1_ref, o_ref, h_ref):
    step = pl.program_id(0)
    steps = h_ref.shape[1] // FBLK

    def fill(gate_ref, up_ref):
        x = x_ref[...]
        hidden = jax.nn.silu(mm(x, gate_ref[...])) * mm(x, up_ref[...])
        h_ref[:, pl.ds(pl.multiple_of(step * FBLK, FBLK), FBLK)] = hidden.astype(jnp.bfloat16)

    @pl.when(step < steps // 2)
    def _():
        fill(g0_ref, u0_ref)

    @pl.when((step >= steps // 2) & (step < steps))
    def _():
        fill(g1_ref, u1_ref)

    @pl.when(step >= steps)
    def _():
        own = d0_ref.shape[0]
        total = mm(h_ref[:, :own], d0_ref[...]) + mm(h_ref[:, own:], d1_ref[...])
        o_ref[...] = total.astype(o_ref.dtype)


def expert_rows(rows, own, other):
    count, width = rows.shape
    hid = own[0].shape[1]
    steps = hid // FBLK
    cols = width // DBLK

    def piece(first, number):
        return lambda i: (0, jnp.clip(i - first, 0, number - 1))

    own_in = pl.BlockSpec((width, FBLK), piece(0, steps))
    other_in = pl.BlockSpec((width, FBLK), piece(steps, steps))
    down_in = pl.BlockSpec((hid, DBLK), piece(2 * steps, cols))
    return pl.pallas_call(
        expert_kernel,
        grid=(2 * steps + cols,),
        in_specs=[pl.BlockSpec((count, width), lambda i: (0, 0)), own_in, other_in, own_in, other_in, down_in, down_in],
        out_specs=pl.BlockSpec((count, DBLK), piece(2 * steps, cols)),
        out_shape=jax.ShapeDtypeStruct((count, width), jnp.bfloat16),
        scratch_shapes=[pltpu.VMEM((count, 2 * hid), jnp.bfloat16)],
        compiler_params=pltpu.CompilerParams(dimension_semantics=("arbitrary",), vmem_limit_bytes=50 << 20),
        cost_estimate=pl.CostEstimate(
            flops=12 * count * width * hid, transcendentals=2 * count * hid, bytes_accessed=12 * width * hid + 4 * count * width
        ),
        name=f"experts_{count}",
    )(rows, own[0], other[0], own[1], other[1], own[2], other[2])


def body(tokens, expert_ids, gate_num, w_gate, w_up, w_down):
    tok, width = tokens.shape
    half = width // 2
    experts = lax.axis_size("expert")
    bf16 = jnp.bfloat16
    own = (w_gate[0], w_up[0], w_down[0])
    other = tuple(lax.ppermute(w, "dp", [(0, 1), (1, 0)]) for w in own)

    ids = expert_ids.T[None]
    hits = ids == jnp.arange(experts, dtype=jnp.int32)[:, None, None]
    member = jnp.any(hits, axis=1)
    numer = jnp.sum(jnp.where(hits, gate_num.T[None], 0), axis=1)
    before = jnp.arange(tok)[:, None] < jnp.arange(tok)[None, :]
    rank_of = mm(member.astype(bf16), before.astype(bf16)).astype(jnp.int32)
    rank_of = jnp.where(member, rank_of, -1)

    main_slot = jnp.arange(MAIN, dtype=jnp.int32)[None, :, None]
    main_place = rank_of[:, None, :] == main_slot
    outgoing = mm(main_place.reshape(experts * MAIN, tok).astype(bf16), tokens).astype(bf16)
    main_in = exchange(outgoing.reshape(experts, MAIN, width))

    line = jnp.arange(2 * EXTRA, dtype=jnp.int32)[None, :, None]
    column_half = jnp.arange(2 * tok, dtype=jnp.int32)[None, None, :] // tok
    rank_twice = jnp.concatenate([rank_of, rank_of], axis=1)[:, None, :]
    extra_place = (rank_twice == MAIN + line % EXTRA) & (line // EXTRA == column_half)
    halves = jnp.concatenate([tokens[:, :half], tokens[:, half:]], axis=0)
    extra_out = mm(extra_place.reshape(experts * 2 * EXTRA, 2 * tok).astype(bf16), halves).astype(bf16)
    extra_out, main_in = lax.optimization_barrier((extra_out, main_in))
    extra_in = exchange(extra_out.reshape(experts, 2 * EXTRA, half))

    main_res = expert_rows(main_in.reshape(experts * MAIN, width), own, other)
    main_back = exchange(main_res.reshape(experts, MAIN, width))

    extra_in, main_res = lax.optimization_barrier((extra_in, main_res))
    count = experts * EXTRA
    row = jnp.arange(count, dtype=jnp.int32)[:, None]
    arrived = jnp.arange(2 * count, dtype=jnp.int32)[None, :]
    at = [(arrived == (row // EXTRA) * 2 * EXTRA + part * EXTRA + row % EXTRA).astype(bf16) for part in (0, 1)]
    pairs = extra_in.reshape(2 * count, half)
    extra_rows = jnp.concatenate([mm(p, pairs).astype(bf16) for p in at], axis=1)
    extra_res = expert_rows(extra_rows, own, other)
    extra_res = (tmm(at[0], extra_res[:, :half]) + tmm(at[1], extra_res[:, half:])).astype(bf16)
    extra_res, main_back = lax.optimization_barrier((extra_res, main_back))
    extra_back = exchange(extra_res.reshape(experts, 2 * EXTRA, half))

    high, low = numer // 8, numer % 8
    main_gate = jnp.concatenate(
        [jnp.where(main_place, part[:, None, :], 0) for part in (high, low)], axis=2
    ).reshape(experts * MAIN, 2 * tok)
    main_sum = tmm(main_gate.astype(bf16), main_back.reshape(experts * MAIN, width))
    extra_gate = jnp.concatenate(
        [jnp.where(extra_place, jnp.concatenate([part, part], axis=1)[:, None, :], 0) for part in (high, low)], axis=2
    ).reshape(experts * 2 * EXTRA, 4 * tok)
    extra_sum = tmm(extra_gate.astype(bf16), extra_back.reshape(experts * 2 * EXTRA, half))
    main_sum = 8.0 * main_sum[:tok] + main_sum[tok:]
    extra_sum = 8.0 * extra_sum[: 2 * tok] + extra_sum[2 * tok :]
    extra_sum = jnp.concatenate([extra_sum[:tok], extra_sum[tok:]], axis=1)
    return ((main_sum + extra_sum) * (1.0 / 1024)).astype(bf16)


def solution(mesh):
    in_specs = (
        P(("dp", "expert"), None),
        P(("dp", "expert"), None),
        P(("dp", "expert"), None),
        P("expert", None, "dp"),
        P("expert", None, "dp"),
        P("expert", "dp", None),
    )
    out_specs = P(("dp", "expert"), None)
    return jax.shard_map(body, mesh=mesh, in_specs=in_specs, out_specs=out_specs, check_vma=False)
```

```python
import jax
import jax.numpy as jnp
from jax import lax
from jax.experimental import pallas as pl
from jax.experimental.pallas import tpu as pltpu
from jax.sharding import PartitionSpec as P

MAIN = 8
EXTRA = 4
FBLK = 256
DBLK = 512
WIDE = 1024
STAGGER = 8000


def mm(a, b):
    return jnp.dot(a, b, preferred_element_type=jnp.float32)


def iota(shape, dim):
    return lax.broadcasted_iota(jnp.int32, shape, dim)


def dispatch_kernel(ids_ref, first_ref, second_ref, o_ref, main_ref, extra_ref):
    step = pl.program_id(0)
    experts, tok = main_ref.shape[0] // MAIN, main_ref.shape[1]

    @pl.when(step == 0)
    def _():
        trips = lax.axis_index("dp") * STAGGER
        spin = lax.fori_loop(0, trips, lambda _, v: v * 0.5, jnp.ones((8, 128), jnp.float32))
        expert = iota((experts, tok), 0)
        member = ids_ref[0:1, :] == expert
        for k in range(1, ids_ref.shape[0]):
            member = member | (ids_ref[k : k + 1, :] == expert)
        before = (iota((tok, tok), 0) < iota((tok, tok), 1)).astype(jnp.float32).astype(jnp.bfloat16)
        rank = mm(jnp.where(member, 1.0, 0.0).astype(jnp.bfloat16), before)
        rank = jnp.where(member, rank, -1.0) + jnp.where(spin[0:1, :tok] > 2.0, 1.0, 0.0)
        shape = (experts, MAIN, tok)
        rank = jnp.broadcast_to(rank[:, None, :], shape)
        line = iota(shape, 1)
        place = jnp.where(rank == line.astype(jnp.float32), 1.0, 0.0)
        main_ref[...] = place.reshape(experts * MAIN, tok).astype(jnp.bfloat16)
        for part in (0, 1):
            slot = jnp.where(line // EXTRA == part, MAIN + line % EXTRA, -2).astype(jnp.float32)
            place = jnp.where(rank == slot, 1.0, 0.0)
            extra_ref[part] = place.reshape(experts * MAIN, tok).astype(jnp.bfloat16)

    blocks = pl.num_programs(0) * 2 // 3

    @pl.when(step < blocks)
    def _():
        o_ref[...] = mm(main_ref[...], first_ref[...]).astype(o_ref.dtype)

    @pl.when(step >= blocks)
    def _():
        o_ref[...] = (mm(extra_ref[0], first_ref[...]) + mm(extra_ref[1], second_ref[...])).astype(o_ref.dtype)


def dispatch(ids, tokens, experts):
    tok, width = tokens.shape
    cols = width // WIDE
    return pl.pallas_call(
        dispatch_kernel,
        grid=(cols * 3 // 2,),
        in_specs=[
            pl.BlockSpec(ids.shape, lambda i: (0, 0)),
            pl.BlockSpec((tok, WIDE), lambda i: (0, jnp.where(i < cols, i, i - cols))),
            pl.BlockSpec((tok, WIDE), lambda i: (0, jnp.maximum(i - cols // 2, cols // 2))),
        ],
        out_specs=pl.BlockSpec((experts * MAIN, WIDE), lambda i: (0, i)),
        out_shape=jax.ShapeDtypeStruct((experts * MAIN, width * 3 // 2), jnp.bfloat16),
        scratch_shapes=[
            pltpu.VMEM((experts * MAIN, tok), jnp.bfloat16),
            pltpu.VMEM((2, experts * MAIN, tok), jnp.bfloat16),
        ],
        compiler_params=pltpu.CompilerParams(dimension_semantics=("arbitrary",)),
        name="dispatch",
    )(ids, tokens, tokens)


def expert_kernel(x_ref, g0_ref, g1_ref, u0_ref, u1_ref, a0_ref, a1_ref, b0_ref, b1_ref, o_ref, rows, halves, hid, out, in_sem, out_sem):
    step = pl.program_id(0)
    steps = hid.shape[1] // FBLK
    main, half = halves.shape
    extra = rows.shape[0] - main
    width = 2 * half
    cols = width // DBLK

    @pl.when(step == 0)
    def _():
        whole = pltpu.make_async_copy(x_ref.at[:, pl.ds(0, width)], rows.at[pl.ds(0, main), :], in_sem.at[0])
        pairs = pltpu.make_async_copy(x_ref.at[:, pl.ds(width, half)], halves, in_sem.at[1])
        pairs.start()
        whole.start()
        pairs.wait()
        row, line = iota((extra, main), 0), iota((extra, main), 1)
        for part in (0, 1):
            take = line == (row // EXTRA) * MAIN + part * EXTRA + row % EXTRA
            take = jnp.where(take, 1.0, 0.0).astype(jnp.bfloat16)
            rows[main:, part * half : (part + 1) * half] = mm(take, halves[...]).astype(jnp.bfloat16)
        whole.wait()

    def fill(gate_ref, up_ref):
        x = rows[...]
        hidden = jax.nn.silu(mm(x, gate_ref[...])) * mm(x, up_ref[...])
        hid[:, pl.ds(pl.multiple_of(step * FBLK, FBLK), FBLK)] = hidden.astype(jnp.bfloat16)

    @pl.when(step < steps // 2)
    def _():
        fill(g0_ref, u0_ref)

    @pl.when((step >= steps // 2) & (step < steps))
    def _():
        fill(g1_ref, u1_ref)

    @pl.when(step >= steps)
    def _():
        own = a0_ref.shape[0]
        q = step - steps
        slot = lax.rem(q, 2)

        def sends(q, slot):
            firsts = (q, q + cols // 2, q + cols)
            return [
                pltpu.make_async_copy(
                    out.at[slot, k], o_ref.at[:, pl.ds(pl.multiple_of(c * DBLK, DBLK), DBLK)], out_sem.at[slot, k]
                )
                for k, c in enumerate(firsts)
            ]

        @pl.when(q >= 2)
        def _():
            for copy in sends(q - 2, slot):
                copy.wait()

        row, line = iota((main, extra), 1), iota((main, extra), 0)
        pair = None
        for part, (d0_ref, d1_ref) in enumerate(((a0_ref, a1_ref), (b0_ref, b1_ref))):
            total = mm(hid[:, :own], d0_ref[...]) + mm(hid[:, own:], d1_ref[...])
            total = total.astype(jnp.bfloat16)
            out[slot, part] = total[:main]
            give = line == (row // EXTRA) * MAIN + part * EXTRA + row % EXTRA
            moved = mm(jnp.where(give, 1.0, 0.0).astype(jnp.bfloat16), total[main:])
            pair = moved if pair is None else pair + moved
        out[slot, 2] = pair.astype(jnp.bfloat16)
        for copy in sends(q, slot):
            copy.start()

        @pl.when(q == cols // 2 - 1)
        def _():
            for copy in sends(q - 1, 1 - slot) + sends(q, slot):
                copy.wait()


def expert_rows(blocks, own, other):
    main, wide = blocks.shape
    width = wide * 2 // 3
    half = width // 2
    count = main * (MAIN + EXTRA) // MAIN
    hid = own[0].shape[1]
    steps = hid // FBLK
    cols = width // DBLK

    def piece(first, number, offset=0):
        return lambda i: (0, jnp.clip(i - first, 0, number - 1) + offset)

    own_in = pl.BlockSpec((width, FBLK), piece(0, steps))
    other_in = pl.BlockSpec((width, FBLK), piece(steps, steps))
    left = pl.BlockSpec((hid, DBLK), piece(2 * steps, cols // 2))
    right = pl.BlockSpec((hid, DBLK), piece(2 * steps, cols // 2, cols // 2))
    return pl.pallas_call(
        expert_kernel,
        grid=(2 * steps + cols // 2,),
        in_specs=[pl.BlockSpec(memory_space=pl.ANY), own_in, other_in, own_in, other_in, left, left, right, right],
        out_specs=pl.BlockSpec(memory_space=pl.ANY),
        out_shape=jax.ShapeDtypeStruct((main, wide), jnp.bfloat16),
        scratch_shapes=[
            pltpu.VMEM((count, width), jnp.bfloat16),
            pltpu.VMEM((main, half), jnp.bfloat16),
            pltpu.VMEM((count, 2 * hid), jnp.bfloat16),
            pltpu.VMEM((2, 3, main, DBLK), jnp.bfloat16),
            pltpu.SemaphoreType.DMA((2,)),
            pltpu.SemaphoreType.DMA((2, 3)),
        ],
        compiler_params=pltpu.CompilerParams(dimension_semantics=("arbitrary",), vmem_limit_bytes=56 << 20),
        cost_estimate=pl.CostEstimate(
            flops=12 * count * width * hid, transcendentals=2 * count * hid, bytes_accessed=12 * width * hid + 4 * main * wide
        ),
        name="experts",
    )(blocks, own[0], other[0], own[1], other[1], own[2], other[2], own[2], other[2])


def combine_kernel(main_ref, extra_ref, whole_ref, pairs_ref, o_ref):
    total = mm(main_ref[...], whole_ref[...]) + mm(extra_ref[0], pairs_ref[...])
    tok = o_ref.shape[0]
    o_ref[...] = ((8.0 * total[:tok] + total[tok:]) * (1.0 / 1024)).astype(o_ref.dtype)


def combine(main_gate, extra_gate, blocks):
    rows, wide = blocks.shape
    width = wide * 2 // 3
    cols = width // WIDE
    tok = main_gate.shape[0] // 2

    def column(i):
        return lax.rem(i, 2) * (cols // 2) + i // 2

    return pl.pallas_call(
        combine_kernel,
        grid=(cols,),
        in_specs=[
            pl.BlockSpec(main_gate.shape, lambda i: (0, 0)),
            pl.BlockSpec((1,) + extra_gate.shape[1:], lambda i: (lax.rem(i, 2), 0, 0)),
            pl.BlockSpec((rows, WIDE), lambda i: (0, column(i))),
            pl.BlockSpec((rows, WIDE), lambda i: (0, cols + i // 2)),
        ],
        out_specs=pl.BlockSpec((tok, WIDE), lambda i: (0, column(i))),
        out_shape=jax.ShapeDtypeStruct((tok, width), jnp.bfloat16),
        compiler_params=pltpu.CompilerParams(dimension_semantics=("arbitrary",)),
        name="combine",
    )(main_gate, extra_gate, blocks, blocks)


def exchange(blocks, experts):
    shape = blocks.shape
    blocks = blocks.reshape(experts, MAIN, shape[1])
    return lax.all_to_all(blocks, "expert", split_axis=0, concat_axis=0, tiled=True).reshape(shape)


def body(tokens, expert_ids, gate_num, w_gate, w_up, w_down):
    tok = tokens.shape[0]
    experts = lax.axis_size("expert")
    bf16 = jnp.bfloat16
    own = (w_gate[0], w_up[0], w_down[0])
    other = tuple(lax.ppermute(w, "dp", [(0, 1), (1, 0)]) for w in own)
    arrived = exchange(dispatch(expert_ids.T, tokens, experts), experts)

    hits = expert_ids[:, :, None] == jnp.arange(experts, dtype=jnp.int32)[None, None, :]
    member = jnp.any(hits, axis=1)
    numer = jnp.sum(jnp.where(hits, gate_num[:, :, None], 0), axis=1)
    after = jnp.arange(tok)[:, None] > jnp.arange(tok)[None, :]
    rank = jnp.where(member, mm(after.astype(bf16), member.astype(bf16)), -1.0)
    spread = (iota((experts, experts * MAIN), 1) // MAIN == iota((experts, experts * MAIN), 0)).astype(bf16)
    line = iota((1, experts * MAIN), 1) % MAIN
    rank_at, high_at, low_at = (mm(v.astype(bf16), spread) for v in (rank, numer // 8, numer % 8))
    both = jnp.concatenate([high_at, low_at], axis=0)
    rank_at = jnp.concatenate([rank_at, rank_at], axis=0)
    main_gate = jnp.where(rank_at == line, both, 0).astype(bf16)
    extra_gate = jnp.stack(
        [
            jnp.where((line // EXTRA == part) & (rank_at == MAIN + line % EXTRA), both, 0).astype(bf16)
            for part in (0, 1)
        ]
    )
    main_gate, extra_gate, arrived = lax.optimization_barrier((main_gate, extra_gate, arrived))

    returned = exchange(expert_rows(arrived, own, other), experts)
    return combine(main_gate, extra_gate, returned)


def solution(mesh):
    in_specs = (
        P(("dp", "expert"), None),
        P(("dp", "expert"), None),
        P(("dp", "expert"), None),
        P("expert", None, "dp"),
        P("expert", None, "dp"),
        P("expert", "dp", None),
    )
    out_specs = P(("dp", "expert"), None)
    return jax.shard_map(body, mesh=mesh, in_specs=in_specs, out_specs=out_specs, check_vma=False)
```

```python
import jax
import jax.numpy as jnp
from jax import lax
from jax.experimental import pallas as pl
from jax.experimental.pallas import tpu as pltpu
from jax.sharding import PartitionSpec as P

MAIN = 8
EXTRA = 4
FBLK = 256
DBLK = 512
WIDE = 1024
STAGGER = (2200, 5500)


def mm(a, b):
    return jnp.dot(a, b, preferred_element_type=jnp.float32)


def tmm(a, b):
    return lax.dot_general(a, b, (((0,), (0,)), ((), ())), preferred_element_type=jnp.float32)


def iota(shape, dim):
    return lax.broadcasted_iota(jnp.int32, shape, dim)


def ranks(ids_ref, experts, tok):
    expert = iota((experts, tok), 0)
    member = ids_ref[0:1, :] == expert
    for k in range(1, ids_ref.shape[0]):
        member = member | (ids_ref[k : k + 1, :] == expert)
    before = (iota((tok, tok), 0) < iota((tok, tok), 1)).astype(jnp.float32).astype(jnp.bfloat16)
    rank = mm(jnp.where(member, 1.0, 0.0).astype(jnp.bfloat16), before)
    return jnp.where(member, rank, -1.0)


def spread(rank):
    experts, tok = rank.shape
    shape = (experts, MAIN, tok)
    return jnp.broadcast_to(rank[:, None, :], shape), iota(shape, 1)


def one_hot(rank, slot):
    place = jnp.where(rank == slot.astype(jnp.float32), 1.0, 0.0)
    return place.reshape(-1, rank.shape[2]).astype(jnp.bfloat16)


def hold_back(rank, trips):
    spin = lax.fori_loop(0, lax.axis_index("dp") * trips, lambda _, v: v * 0.5, jnp.ones((8, 128), jnp.float32))
    return rank + jnp.where(spin[0:1, : rank.shape[1]] > 2.0, 1.0, 0.0)


def main_kernel(ids_ref, tokens_ref, o_ref, place_ref):
    @pl.when(pl.program_id(0) == 0)
    def _():
        rank = ranks(ids_ref, place_ref.shape[0] // MAIN, place_ref.shape[1])
        rank, line = spread(hold_back(rank, STAGGER[1]))
        place_ref[...] = one_hot(rank, line)

    o_ref[...] = mm(place_ref[...], tokens_ref[...]).astype(o_ref.dtype)


def extra_kernel(ids_ref, first_ref, second_ref, o_ref, place_ref):
    tok = first_ref.shape[0]

    @pl.when(pl.program_id(0) == 0)
    def _():
        rank, line = spread(hold_back(ranks(ids_ref, place_ref.shape[0] // MAIN, tok), STAGGER[0]))
        for part in (0, 1):
            slot = jnp.where(line // EXTRA == part, MAIN + line % EXTRA, -2)
            place_ref[:, part * tok : (part + 1) * tok] = one_hot(rank, slot)

    both = jnp.concatenate([first_ref[...], second_ref[...]], axis=0)
    o_ref[...] = mm(place_ref[...], both).astype(o_ref.dtype)


def dispatch(kernel, parts, ids, tokens, experts, name):
    tok, width = tokens.shape
    rows, cols = experts * MAIN, width // parts // WIDE
    return pl.pallas_call(
        kernel,
        grid=(cols,),
        in_specs=[pl.BlockSpec(ids.shape, lambda i: (0, 0))]
        + [pl.BlockSpec((tok, WIDE), lambda i, first=first: (0, first * cols + i)) for first in range(parts)],
        out_specs=pl.BlockSpec((rows, WIDE), lambda i: (0, i)),
        out_shape=jax.ShapeDtypeStruct((rows, width // parts), jnp.bfloat16),
        scratch_shapes=[pltpu.VMEM((rows, parts * tok), jnp.bfloat16)],
        compiler_params=pltpu.CompilerParams(dimension_semantics=("arbitrary",)),
        name=name,
    )(ids, *[tokens] * parts)


def expert_kernel(x_ref, g0_ref, g1_ref, u0_ref, u1_ref, d0_ref, d1_ref, o_ref, h_ref):
    step = pl.program_id(0)
    steps = h_ref.shape[1] // FBLK

    def fill(gate_ref, up_ref):
        x = x_ref[...]
        hidden = jax.nn.silu(mm(x, gate_ref[...])) * mm(x, up_ref[...])
        h_ref[:, pl.ds(pl.multiple_of(step * FBLK, FBLK), FBLK)] = hidden.astype(jnp.bfloat16)

    @pl.when(step < steps // 2)
    def _():
        fill(g0_ref, u0_ref)

    @pl.when((step >= steps // 2) & (step < steps))
    def _():
        fill(g1_ref, u1_ref)

    @pl.when(step >= steps)
    def _():
        own = d0_ref.shape[0]
        total = mm(h_ref[:, :own], d0_ref[...]) + mm(h_ref[:, own:], d1_ref[...])
        o_ref[...] = total.astype(o_ref.dtype)


def expert_rows(rows, own, other):
    count, width = rows.shape
    hid = own[0].shape[1]
    steps = hid // FBLK
    cols = width // DBLK

    def piece(first, number):
        return lambda i: (0, jnp.clip(i - first, 0, number - 1))

    own_in = pl.BlockSpec((width, FBLK), piece(0, steps))
    other_in = pl.BlockSpec((width, FBLK), piece(steps, steps))
    down_in = pl.BlockSpec((hid, DBLK), piece(2 * steps, cols))
    return pl.pallas_call(
        expert_kernel,
        grid=(2 * steps + cols,),
        in_specs=[pl.BlockSpec((count, width), lambda i: (0, 0)), own_in, other_in, own_in, other_in, down_in, down_in],
        out_specs=pl.BlockSpec((count, DBLK), piece(2 * steps, cols)),
        out_shape=jax.ShapeDtypeStruct((count, width), jnp.bfloat16),
        scratch_shapes=[pltpu.VMEM((count, 2 * hid), jnp.bfloat16)],
        compiler_params=pltpu.CompilerParams(dimension_semantics=("arbitrary",), vmem_limit_bytes=50 << 20),
        cost_estimate=pl.CostEstimate(
            flops=12 * count * width * hid, transcendentals=2 * count * hid, bytes_accessed=12 * width * hid + 4 * count * width
        ),
        name=f"experts_{count}",
    )(rows, own[0], other[0], own[1], other[1], own[2], other[2])


def combine_kernel(main_ref, extra_ref, left_ref, right_ref, pairs_ref, o_ref):
    tok, width = o_ref.shape
    step = pl.program_id(0)
    pairs = mm(extra_ref[...], pairs_ref[...])
    for part, whole_ref in enumerate((left_ref, right_ref)):
        total = mm(main_ref[...], whole_ref[...]) + pairs[part * 2 * tok : (part + 1) * 2 * tok]
        first = pl.multiple_of(part * (width // 2) + step * WIDE, WIDE)
        o_ref[:, pl.ds(first, WIDE)] = ((8.0 * total[:tok] + total[tok:]) * (1.0 / 1024)).astype(o_ref.dtype)


def combine(main_gate, extra_gate, whole, pairs):
    rows, width = whole.shape
    cols = width // 2 // WIDE
    tok = main_gate.shape[0] // 2
    return pl.pallas_call(
        combine_kernel,
        grid=(cols,),
        in_specs=[
            pl.BlockSpec(main_gate.shape, lambda i: (0, 0)),
            pl.BlockSpec(extra_gate.shape, lambda i: (0, 0)),
            pl.BlockSpec((rows, WIDE), lambda i: (0, i)),
            pl.BlockSpec((rows, WIDE), lambda i: (0, cols + i)),
            pl.BlockSpec((rows, WIDE), lambda i: (0, i)),
        ],
        out_specs=pl.BlockSpec((tok, width), lambda i: (0, 0)),
        out_shape=jax.ShapeDtypeStruct((tok, width), jnp.bfloat16),
        compiler_params=pltpu.CompilerParams(dimension_semantics=("arbitrary",)),
        name="combine",
    )(main_gate, extra_gate, whole, whole, pairs)


def exchange(blocks, experts):
    shape = blocks.shape
    blocks = blocks.reshape(experts, MAIN, shape[1])
    return lax.all_to_all(blocks, "expert", split_axis=0, concat_axis=0, tiled=True).reshape(shape)


def body(tokens, expert_ids, gate_num, w_gate, w_up, w_down):
    tok = tokens.shape[0]
    experts = lax.axis_size("expert")
    bf16 = jnp.bfloat16
    own = (w_gate[0], w_up[0], w_down[0])
    other = tuple(lax.ppermute(w, "dp", [(0, 1), (1, 0)]) for w in own)
    extra_out = dispatch(extra_kernel, 2, expert_ids.T, tokens, experts, "dispatch_extra")
    extra_in = exchange(extra_out, experts)
    main_out = dispatch(main_kernel, 1, expert_ids.T, tokens, experts, "dispatch_main")
    main_out, extra_in = lax.optimization_barrier((main_out, extra_in))
    main_in = exchange(main_out, experts)

    hits = expert_ids[:, :, None] == jnp.arange(experts, dtype=jnp.int32)[None, None, :]
    member = jnp.any(hits, axis=1)
    numer = jnp.sum(jnp.where(hits, gate_num[:, :, None], 0), axis=1)
    after = jnp.arange(tok)[:, None] > jnp.arange(tok)[None, :]
    rank = jnp.where(member, mm(after.astype(bf16), member.astype(bf16)), -1.0)
    slots = (iota((experts, experts * MAIN), 1) // MAIN == iota((experts, experts * MAIN), 0)).astype(bf16)
    line = iota((1, experts * MAIN), 1) % MAIN
    rank_at, high_at, low_at = (mm(v.astype(bf16), slots) for v in (rank, numer // 8, numer % 8))
    both = jnp.concatenate([high_at, low_at], axis=0)
    rank_at = jnp.concatenate([rank_at, rank_at], axis=0)
    main_gate = jnp.where(rank_at == line, both, 0).astype(bf16)
    extra_gate = jnp.concatenate(
        [
            jnp.where((line // EXTRA == part) & (rank_at == MAIN + line % EXTRA), both, 0).astype(bf16)
            for part in (0, 1)
        ]
    )

    count, half = experts * EXTRA, tokens.shape[1] // 2
    row, line = iota((count, 2 * count), 0), iota((count, 2 * count), 1)
    at = [(line == (row // EXTRA) * MAIN + part * EXTRA + row % EXTRA).astype(bf16) for part in (0, 1)]
    main_gate, extra_gate, extra_in = lax.optimization_barrier((main_gate, extra_gate, extra_in))
    extra_rows = jnp.concatenate([mm(p, extra_in).astype(bf16) for p in at], axis=1)
    extra_res = expert_rows(extra_rows, own, other)
    extra_res = (tmm(at[0], extra_res[:, :half]) + tmm(at[1], extra_res[:, half:])).astype(bf16)
    extra_res, main_in = lax.optimization_barrier((extra_res, main_in))
    extra_back = exchange(extra_res, experts)
    main_res = expert_rows(main_in, own, other)
    main_res, extra_back = lax.optimization_barrier((main_res, extra_back))
    main_back = exchange(main_res, experts)
    return combine(main_gate, extra_gate, main_back, extra_back)


def solution(mesh):
    in_specs = (
        P(("dp", "expert"), None),
        P(("dp", "expert"), None),
        P(("dp", "expert"), None),
        P("expert", None, "dp"),
        P("expert", None, "dp"),
        P("expert", "dp", None),
    )
    out_specs = P(("dp", "expert"), None)
    return jax.shard_map(body, mesh=mesh, in_specs=in_specs, out_specs=out_specs, check_vma=False)
```

```python
import jax
import jax.numpy as jnp
from jax import lax
from jax.experimental import pallas as pl
from jax.experimental.pallas import tpu as pltpu
from jax.sharding import PartitionSpec as P

MAIN = 8
EXTRA = 4
FBLK = 256
DBLK = 512
WIDE = 1024
STAGGER = (2800, 3650)


def mm(a, b):
    return jnp.dot(a, b, preferred_element_type=jnp.float32)


def tmm(a, b):
    return lax.dot_general(a, b, (((0,), (0,)), ((), ())), preferred_element_type=jnp.float32)


def iota(shape, dim):
    return lax.broadcasted_iota(jnp.int32, shape, dim)


def ranks(ids_ref, experts, tok):
    expert = iota((experts, tok), 0)
    member = ids_ref[0:1, :] == expert
    for k in range(1, ids_ref.shape[0]):
        member = member | (ids_ref[k : k + 1, :] == expert)
    before = (iota((tok, tok), 0) < iota((tok, tok), 1)).astype(jnp.float32).astype(jnp.bfloat16)
    rank = mm(jnp.where(member, 1.0, 0.0).astype(jnp.bfloat16), before)
    return jnp.where(member, rank, -1.0)


def spread(rank):
    experts, tok = rank.shape
    shape = (experts, MAIN, tok)
    return jnp.broadcast_to(rank[:, None, :], shape), iota(shape, 1)


def one_hot(rank, slot):
    place = jnp.where(rank == slot.astype(jnp.float32), 1.0, 0.0)
    return place.reshape(-1, rank.shape[2]).astype(jnp.bfloat16)


def hold_back(rank, trips):
    spin = lax.fori_loop(0, lax.axis_index("dp") * trips, lambda _, v: v * 0.5, jnp.ones((8, 128), jnp.float32))
    return rank + jnp.where(spin[0:1, : rank.shape[1]] > 2.0, 1.0, 0.0)


def main_kernel(ids_ref, tokens_ref, o_ref, place_ref):
    @pl.when(pl.program_id(0) == 0)
    def _():
        rank = ranks(ids_ref, place_ref.shape[0] // MAIN, place_ref.shape[1])
        rank, line = spread(hold_back(rank, STAGGER[1]))
        place_ref[...] = one_hot(rank, line)

    o_ref[...] = mm(place_ref[...], tokens_ref[...]).astype(o_ref.dtype)


def extra_kernel(ids_ref, first_ref, second_ref, o_ref, place_ref):
    tok = first_ref.shape[0]

    @pl.when(pl.program_id(0) == 0)
    def _():
        rank, line = spread(hold_back(ranks(ids_ref, place_ref.shape[0] // MAIN, tok), STAGGER[0]))
        for part in (0, 1):
            slot = jnp.where(line // EXTRA == part, MAIN + line % EXTRA, -2)
            place_ref[:, part * tok : (part + 1) * tok] = one_hot(rank, slot)

    both = jnp.concatenate([first_ref[...], second_ref[...]], axis=0)
    o_ref[...] = mm(place_ref[...], both).astype(o_ref.dtype)


def dispatch(kernel, parts, ids, tokens, experts, name):
    tok, width = tokens.shape
    rows, cols = experts * MAIN, width // parts // WIDE
    return pl.pallas_call(
        kernel,
        grid=(cols,),
        in_specs=[pl.BlockSpec(ids.shape, lambda i: (0, 0))]
        + [pl.BlockSpec((tok, WIDE), lambda i, first=first: (0, first * cols + i)) for first in range(parts)],
        out_specs=pl.BlockSpec((rows, WIDE), lambda i: (0, i)),
        out_shape=jax.ShapeDtypeStruct((rows, width // parts), jnp.bfloat16),
        scratch_shapes=[pltpu.VMEM((rows, parts * tok), jnp.bfloat16)],
        compiler_params=pltpu.CompilerParams(dimension_semantics=("arbitrary",)),
        name=name,
    )(ids, *[tokens] * parts)


def expert_kernel(x_ref, g0_ref, g1_ref, u0_ref, u1_ref, d0_ref, d1_ref, o_ref, h_ref):
    step = pl.program_id(0)
    steps = h_ref.shape[1] // FBLK

    def fill(gate_ref, up_ref):
        x = x_ref[...]
        hidden = jax.nn.silu(mm(x, gate_ref[...])) * mm(x, up_ref[...])
        h_ref[:, pl.ds(pl.multiple_of(step * FBLK, FBLK), FBLK)] = hidden.astype(jnp.bfloat16)

    @pl.when(step < steps // 2)
    def _():
        fill(g0_ref, u0_ref)

    @pl.when((step >= steps // 2) & (step < steps))
    def _():
        fill(g1_ref, u1_ref)

    @pl.when(step >= steps)
    def _():
        own = d0_ref.shape[0]
        total = mm(h_ref[:, :own], d0_ref[...]) + mm(h_ref[:, own:], d1_ref[...])
        o_ref[...] = total.astype(o_ref.dtype)


def expert_rows(rows, own, other):
    count, width = rows.shape
    hid = own[0].shape[1]
    steps = hid // FBLK
    cols = width // DBLK

    def piece(first, number):
        return lambda i: (0, jnp.clip(i - first, 0, number - 1))

    own_in = pl.BlockSpec((width, FBLK), piece(0, steps))
    other_in = pl.BlockSpec((width, FBLK), piece(steps, steps))
    down_in = pl.BlockSpec((hid, DBLK), piece(2 * steps, cols))
    return pl.pallas_call(
        expert_kernel,
        grid=(2 * steps + cols,),
        in_specs=[pl.BlockSpec((count, width), lambda i: (0, 0)), own_in, other_in, own_in, other_in, down_in, down_in],
        out_specs=pl.BlockSpec((count, DBLK), piece(2 * steps, cols)),
        out_shape=jax.ShapeDtypeStruct((count, width), jnp.bfloat16),
        scratch_shapes=[pltpu.VMEM((count, 2 * hid), jnp.bfloat16)],
        compiler_params=pltpu.CompilerParams(dimension_semantics=("arbitrary",), vmem_limit_bytes=50 << 20),
        cost_estimate=pl.CostEstimate(
            flops=12 * count * width * hid, transcendentals=2 * count * hid, bytes_accessed=12 * width * hid + 4 * count * width
        ),
        name=f"experts_{count}",
    )(rows, own[0], other[0], own[1], other[1], own[2], other[2])


def combine_kernel(main_ref, extra_ref, left_ref, right_ref, pairs_ref, o_ref):
    tok, width = o_ref.shape
    step = pl.program_id(0)
    pairs = mm(extra_ref[...], pairs_ref[...])
    for part, whole_ref in enumerate((left_ref, right_ref)):
        total = mm(main_ref[...], whole_ref[...]) + pairs[part * 2 * tok : (part + 1) * 2 * tok]
        first = pl.multiple_of(part * (width // 2) + step * WIDE, WIDE)
        o_ref[:, pl.ds(first, WIDE)] = ((8.0 * total[:tok] + total[tok:]) * (1.0 / 1024)).astype(o_ref.dtype)


def combine(main_gate, extra_gate, whole, pairs):
    rows, width = whole.shape
    cols = width // 2 // WIDE
    tok = main_gate.shape[0] // 2
    return pl.pallas_call(
        combine_kernel,
        grid=(cols,),
        in_specs=[
            pl.BlockSpec(main_gate.shape, lambda i: (0, 0)),
            pl.BlockSpec(extra_gate.shape, lambda i: (0, 0)),
            pl.BlockSpec((rows, WIDE), lambda i: (0, i)),
            pl.BlockSpec((rows, WIDE), lambda i: (0, cols + i)),
            pl.BlockSpec((rows, WIDE), lambda i: (0, i)),
        ],
        out_specs=pl.BlockSpec((tok, width), lambda i: (0, 0)),
        out_shape=jax.ShapeDtypeStruct((tok, width), jnp.bfloat16),
        compiler_params=pltpu.CompilerParams(dimension_semantics=("arbitrary",)),
        name="combine",
    )(main_gate, extra_gate, whole, whole, pairs)


def exchange(blocks, experts):
    shape = blocks.shape
    blocks = blocks.reshape(experts, MAIN, shape[1])
    return lax.all_to_all(blocks, "expert", split_axis=0, concat_axis=0, tiled=True).reshape(shape)


def body(tokens, expert_ids, gate_num, w_gate, w_up, w_down):
    tok = tokens.shape[0]
    experts = lax.axis_size("expert")
    bf16 = jnp.bfloat16
    own = (w_gate[0], w_up[0], w_down[0])
    other = tuple(lax.ppermute(w, "dp", [(0, 1), (1, 0)]) for w in own)
    extra_out = dispatch(extra_kernel, 2, expert_ids.T, tokens, experts, "dispatch_extra")
    extra_in = exchange(extra_out, experts)
    main_out = dispatch(main_kernel, 1, expert_ids.T, tokens, experts, "dispatch_main")

    hits = expert_ids[:, :, None] == jnp.arange(experts, dtype=jnp.int32)[None, None, :]
    member = jnp.any(hits, axis=1)
    numer = jnp.sum(jnp.where(hits, gate_num[:, :, None], 0), axis=1)
    after = jnp.arange(tok)[:, None] > jnp.arange(tok)[None, :]
    rank = jnp.where(member, mm(after.astype(bf16), member.astype(bf16)), -1.0)
    slots = (iota((experts, experts * MAIN), 1) // MAIN == iota((experts, experts * MAIN), 0)).astype(bf16)
    line = iota((1, experts * MAIN), 1) % MAIN
    rank_at, high_at, low_at = (mm(v.astype(bf16), slots) for v in (rank, numer // 8, numer % 8))
    both = jnp.concatenate([high_at, low_at], axis=0)
    rank_at = jnp.concatenate([rank_at, rank_at], axis=0)
    main_gate = jnp.where(rank_at == line, both, 0).astype(bf16)
    extra_gate = jnp.concatenate(
        [
            jnp.where((line // EXTRA == part) & (rank_at == MAIN + line % EXTRA), both, 0).astype(bf16)
            for part in (0, 1)
        ]
    )

    count, half = experts * EXTRA, tokens.shape[1] // 2
    row, line = iota((count, 2 * count), 0), iota((count, 2 * count), 1)
    at = [(line == (row // EXTRA) * MAIN + part * EXTRA + row % EXTRA).astype(bf16) for part in (0, 1)]
    main_out, main_gate, extra_gate, extra_in = lax.optimization_barrier((main_out, main_gate, extra_gate, extra_in))
    main_in = exchange(main_out, experts)
    extra_rows = jnp.concatenate([mm(p, extra_in).astype(bf16) for p in at], axis=1)
    extra_res = expert_rows(extra_rows, own, other)
    extra_res = (tmm(at[0], extra_res[:, :half]) + tmm(at[1], extra_res[:, half:])).astype(bf16)
    extra_res, main_in = lax.optimization_barrier((extra_res, main_in))
    extra_back = exchange(extra_res, experts)
    main_res = expert_rows(main_in, own, other)
    main_res, extra_back = lax.optimization_barrier((main_res, extra_back))
    main_back = exchange(main_res, experts)
    return combine(main_gate, extra_gate, main_back, extra_back)


def solution(mesh):
    in_specs = (
        P(("dp", "expert"), None),
        P(("dp", "expert"), None),
        P(("dp", "expert"), None),
        P("expert", None, "dp"),
        P("expert", None, "dp"),
        P("expert", "dp", None),
    )
    out_specs = P(("dp", "expert"), None)
    return jax.shard_map(body, mesh=mesh, in_specs=in_specs, out_specs=out_specs, check_vma=False)
```

```python
import jax
import jax.numpy as jnp
from jax import lax
from jax.experimental import pallas as pl
from jax.experimental.pallas import tpu as pltpu
from jax.sharding import PartitionSpec as P

MAIN = 8
EXTRA = 4
FBLK = 256
DBLK = 512
WIDE = 1024
NARROW = 512
STAGGER = (2800, 3650)


def mm(a, b):
    return jnp.dot(a, b, preferred_element_type=jnp.float32)


def tmm(a, b):
    return lax.dot_general(a, b, (((0,), (0,)), ((), ())), preferred_element_type=jnp.float32)


def iota(shape, dim):
    return lax.broadcasted_iota(jnp.int32, shape, dim)


def ranks(ids_ref, experts, tok):
    expert = iota((experts, tok), 0)
    member = ids_ref[0:1, :] == expert
    for k in range(1, ids_ref.shape[0]):
        member = member | (ids_ref[k : k + 1, :] == expert)
    before = (iota((tok, tok), 0) < iota((tok, tok), 1)).astype(jnp.float32).astype(jnp.bfloat16)
    rank = mm(jnp.where(member, 1.0, 0.0).astype(jnp.bfloat16), before)
    return jnp.where(member, rank, -1.0)


def spread(rank):
    experts, tok = rank.shape
    shape = (experts, MAIN, tok)
    return jnp.broadcast_to(rank[:, None, :], shape), iota(shape, 1)


def one_hot(rank, slot):
    place = jnp.where(rank == slot.astype(jnp.float32), 1.0, 0.0)
    return place.reshape(-1, rank.shape[2]).astype(jnp.bfloat16)


def hold_back(rank, trips):
    spin = lax.fori_loop(0, lax.axis_index("dp") * trips, lambda _, v: v * 0.5, jnp.ones((8, 128), jnp.float32))
    return rank + jnp.where(spin[0:1, : rank.shape[1]] > 2.0, 1.0, 0.0)


def main_kernel(ids_ref, tokens_ref, o_ref, place_ref):
    @pl.when(pl.program_id(0) == 0)
    def _():
        rank = ranks(ids_ref, place_ref.shape[0] // MAIN, place_ref.shape[1])
        rank, line = spread(hold_back(rank, STAGGER[1]))
        place_ref[...] = one_hot(rank, line)

    o_ref[...] = mm(place_ref[...], tokens_ref[...]).astype(o_ref.dtype)


def extra_kernel(ids_ref, first_ref, second_ref, o_ref, place_ref):
    tok = first_ref.shape[0]

    @pl.when(pl.program_id(0) == 0)
    def _():
        rank, line = spread(hold_back(ranks(ids_ref, place_ref.shape[0] // MAIN, tok), STAGGER[0]))
        for part in (0, 1):
            slot = jnp.where(line // EXTRA == part, MAIN + line % EXTRA, -2)
            place_ref[:, part * tok : (part + 1) * tok] = one_hot(rank, slot)

    both = jnp.concatenate([first_ref[...], second_ref[...]], axis=0)
    o_ref[...] = mm(place_ref[...], both).astype(o_ref.dtype)


def dispatch(kernel, parts, ids, tokens, experts, name):
    tok, width = tokens.shape
    rows, cols = experts * MAIN, width // parts // WIDE
    return pl.pallas_call(
        kernel,
        grid=(cols,),
        in_specs=[pl.BlockSpec(ids.shape, lambda i: (0, 0))]
        + [pl.BlockSpec((tok, WIDE), lambda i, first=first: (0, first * cols + i)) for first in range(parts)],
        out_specs=pl.BlockSpec((rows, WIDE), lambda i: (0, i)),
        out_shape=jax.ShapeDtypeStruct((rows, width // parts), jnp.bfloat16),
        scratch_shapes=[pltpu.VMEM((rows, parts * tok), jnp.bfloat16)],
        compiler_params=pltpu.CompilerParams(dimension_semantics=("arbitrary",)),
        name=name,
    )(ids, *[tokens] * parts)


def expert_kernel(x_ref, g0_ref, g1_ref, u0_ref, u1_ref, d0_ref, d1_ref, o_ref, h_ref):
    step = pl.program_id(0)
    steps = h_ref.shape[1] // FBLK

    def fill(gate_ref, up_ref):
        x = x_ref[...]
        hidden = jax.nn.silu(mm(x, gate_ref[...])) * mm(x, up_ref[...])
        h_ref[:, pl.ds(pl.multiple_of(step * FBLK, FBLK), FBLK)] = hidden.astype(jnp.bfloat16)

    @pl.when(step < steps // 2)
    def _():
        fill(g0_ref, u0_ref)

    @pl.when((step >= steps // 2) & (step < steps))
    def _():
        fill(g1_ref, u1_ref)

    @pl.when(step >= steps)
    def _():
        own = d0_ref.shape[0]
        total = mm(h_ref[:, :own], d0_ref[...]) + mm(h_ref[:, own:], d1_ref[...])
        o_ref[...] = total.astype(o_ref.dtype)


def expert_rows(rows, own, other):
    count, width = rows.shape
    hid = own[0].shape[1]
    steps = hid // FBLK
    cols = width // DBLK

    def piece(first, number):
        return lambda i: (0, jnp.clip(i - first, 0, number - 1))

    own_in = pl.BlockSpec((width, FBLK), piece(0, steps))
    other_in = pl.BlockSpec((width, FBLK), piece(steps, steps))
    down_in = pl.BlockSpec((hid, DBLK), piece(2 * steps, cols))
    return pl.pallas_call(
        expert_kernel,
        grid=(2 * steps + cols,),
        in_specs=[pl.BlockSpec((count, width), lambda i: (0, 0)), own_in, other_in, own_in, other_in, down_in, down_in],
        out_specs=pl.BlockSpec((count, DBLK), piece(2 * steps, cols)),
        out_shape=jax.ShapeDtypeStruct((count, width), jnp.bfloat16),
        scratch_shapes=[pltpu.VMEM((count, 2 * hid), jnp.bfloat16)],
        compiler_params=pltpu.CompilerParams(dimension_semantics=("arbitrary",), vmem_limit_bytes=50 << 20),
        cost_estimate=pl.CostEstimate(
            flops=12 * count * width * hid, transcendentals=2 * count * hid, bytes_accessed=12 * width * hid + 4 * count * width
        ),
        name=f"experts_{count}",
    )(rows, own[0], other[0], own[1], other[1], own[2], other[2])


def combine_kernel(main_ref, extra_ref, left_ref, right_ref, pairs_ref, o_ref):
    tok, width = o_ref.shape
    step = pl.program_id(0)
    pairs = mm(extra_ref[...], pairs_ref[...])
    for part, whole_ref in enumerate((left_ref, right_ref)):
        total = mm(main_ref[...], whole_ref[...]) + pairs[part * 2 * tok : (part + 1) * 2 * tok]
        first = pl.multiple_of(part * (width // 2) + step * NARROW, NARROW)
        o_ref[:, pl.ds(first, NARROW)] = ((8.0 * total[:tok] + total[tok:]) * (1.0 / 1024)).astype(o_ref.dtype)


def combine(main_gate, extra_gate, whole, pairs):
    rows, width = whole.shape
    cols = width // 2 // NARROW
    tok = main_gate.shape[0] // 2
    return pl.pallas_call(
        combine_kernel,
        grid=(cols,),
        in_specs=[
            pl.BlockSpec(main_gate.shape, lambda i: (0, 0)),
            pl.BlockSpec(extra_gate.shape, lambda i: (0, 0)),
            pl.BlockSpec((rows, NARROW), lambda i: (0, i)),
            pl.BlockSpec((rows, NARROW), lambda i: (0, cols + i)),
            pl.BlockSpec((rows, NARROW), lambda i: (0, i)),
        ],
        out_specs=pl.BlockSpec((tok, width), lambda i: (0, 0)),
        out_shape=jax.ShapeDtypeStruct((tok, width), jnp.bfloat16),
        compiler_params=pltpu.CompilerParams(dimension_semantics=("arbitrary",)),
        name="combine",
    )(main_gate, extra_gate, whole, whole, pairs)


def exchange(blocks, experts):
    shape = blocks.shape
    blocks = blocks.reshape(experts, MAIN, shape[1])
    return lax.all_to_all(blocks, "expert", split_axis=0, concat_axis=0, tiled=True).reshape(shape)


def body(tokens, expert_ids, gate_num, w_gate, w_up, w_down):
    tok = tokens.shape[0]
    experts = lax.axis_size("expert")
    bf16 = jnp.bfloat16
    own = (w_gate[0], w_up[0], w_down[0])
    other = tuple(lax.ppermute(w, "dp", [(0, 1), (1, 0)]) for w in own)
    extra_out = dispatch(extra_kernel, 2, expert_ids.T, tokens, experts, "dispatch_extra")
    extra_in = exchange(extra_out, experts)
    main_out = dispatch(main_kernel, 1, expert_ids.T, tokens, experts, "dispatch_main")

    hits = expert_ids[:, :, None] == jnp.arange(experts, dtype=jnp.int32)[None, None, :]
    member = jnp.any(hits, axis=1)
    numer = jnp.sum(jnp.where(hits, gate_num[:, :, None], 0), axis=1)
    after = jnp.arange(tok)[:, None] > jnp.arange(tok)[None, :]
    rank = jnp.where(member, mm(after.astype(bf16), member.astype(bf16)), -1.0)
    slots = (iota((experts, experts * MAIN), 1) // MAIN == iota((experts, experts * MAIN), 0)).astype(bf16)
    line = iota((1, experts * MAIN), 1) % MAIN
    rank_at, high_at, low_at = (mm(v.astype(bf16), slots) for v in (rank, numer // 8, numer % 8))
    both = jnp.concatenate([high_at, low_at], axis=0)
    rank_at = jnp.concatenate([rank_at, rank_at], axis=0)
    main_gate = jnp.where(rank_at == line, both, 0).astype(bf16)
    extra_gate = jnp.concatenate(
        [
            jnp.where((line // EXTRA == part) & (rank_at == MAIN + line % EXTRA), both, 0).astype(bf16)
            for part in (0, 1)
        ]
    )

    count, half = experts * EXTRA, tokens.shape[1] // 2
    row, line = iota((count, 2 * count), 0), iota((count, 2 * count), 1)
    at = [(line == (row // EXTRA) * MAIN + part * EXTRA + row % EXTRA).astype(bf16) for part in (0, 1)]
    main_out, main_gate, extra_gate, extra_in = lax.optimization_barrier((main_out, main_gate, extra_gate, extra_in))
    main_in = exchange(main_out, experts)
    extra_rows = jnp.concatenate([mm(p, extra_in).astype(bf16) for p in at], axis=1)
    extra_res = expert_rows(extra_rows, own, other)
    extra_res = (tmm(at[0], extra_res[:, :half]) + tmm(at[1], extra_res[:, half:])).astype(bf16)
    extra_res, main_in = lax.optimization_barrier((extra_res, main_in))
    extra_back = exchange(extra_res, experts)
    main_res = expert_rows(main_in, own, other)
    main_res, extra_back = lax.optimization_barrier((main_res, extra_back))
    main_back = exchange(main_res, experts)
    return combine(main_gate, extra_gate, main_back, extra_back)


def solution(mesh):
    in_specs = (
        P(("dp", "expert"), None),
        P(("dp", "expert"), None),
        P(("dp", "expert"), None),
        P("expert", None, "dp"),
        P("expert", None, "dp"),
        P("expert", "dp", None),
    )
    out_specs = P(("dp", "expert"), None)
    return jax.shard_map(body, mesh=mesh, in_specs=in_specs, out_specs=out_specs, check_vma=False)
```
